32 devices in a mesh: row: 4 (over y, core), blk: 8 (over z, x).
Axes of the slice: x: 2, y: 2, z: 4, core: 2. Of those that a mesh axis runs over, the one named last changes fastest.
Arguments:
- theta: float32 [8, 8, 256, 256], P('blk'), may hold values from -6 to 6
- left_env: float32 [16, 8, 256, 256], P('row', 'blk'), may hold values from -0.375 to 0.375
- right_env: float32 [16, 8, 256, 256], P('row', 'blk'), may hold values from -0.375 to 0.375
- left_tiles: int32 [8], replicated, may hold values from 1 to 4
- right_tiles: int32 [8], replicated, may hold values from 1 to 4
- pairs: int32 [48, 2], replicated, may hold values from 0 to 15
- coefs: float32 [48], replicated, may hold values from -2 to 2
Outputs:
- hpsi: float32 [8, 8, 256, 256], P('blk', None, 'row')
The draws below stay inside these ranges and needn't reach their ends.
All inputs are finite; a program needn't handle non-finite values.
Results may differ from the reference program's by a relative error of at most 0.000071.
Values sent between devices are 32-bit elements; how exact they have to be, the bound alone decides.
No kernel may reach another device: no remote copies, remote signals or barrier semaphores. Data moves between devices by JAX's collectives and lax.ppermute only.
A program may use at most 128 MiB of HBM per device.

```python
import jax
import jax.numpy as jnp
from jax import lax

MB = 256
NW = 16
KP = 48
NP = 8
NQ = 8


def with_ends(entries, own_key, low, largest):
    index_at = [jax.random.randint(jax.random.fold_in(own_key, axis), (), 0, length) for axis, length in enumerate(entries.shape)]
    main_axis = entries.shape.index(max(entries.shape))
    beside = index_at[:main_axis] + [(index_at[main_axis] + 1) % entries.shape[main_axis]] + index_at[main_axis + 1:]
    return entries.at[tuple(index_at)].set(low).at[tuple(beside)].set(largest)


def block_levels(stream_key, extent, cuts, low, top_value):
    def one(position, blocks):
        draws = jax.random.uniform(jax.random.fold_in(jax.random.fold_in(stream_key, 6), position), (blocks,), jnp.float32, low / len(cuts), top_value / len(cuts))
        return jnp.repeat(jnp.exp(draws), extent[position] // blocks).reshape((-1,) + (1,) * (len(extent) - position - 1))

    loudness = one(*cuts[0])
    for cut in cuts[1:]:
        loudness = loudness * one(*cut)
    return loudness


def bell_draw(rng, shape, deviation, bound, split=(), kind=jnp.bfloat16):
    loudness = block_levels(rng, shape, split, -0.22, 0.18) if split else 1.0
    drawn = jax.random.normal(rng, shape, jnp.float32) * deviation * loudness
    return jnp.minimum(jnp.maximum(drawn, -bound), bound).astype(kind)


def setup_inputs(seed: int = 0) -> dict:
    streams_of = jax.random.split(jax.random.key(seed), 8)
    return {
        "theta": bell_draw(streams_of[0], (NP, NQ, MB, MB), 1.0, 6.0, ((0, 8),), jnp.float32),
        "left_env": bell_draw(streams_of[1], (NW, NP, MB, MB), MB ** -0.5, 0.375, ((0, 4), (1, 8)), jnp.float32),
        "right_env": bell_draw(streams_of[2], (NW, NQ, MB, MB), MB ** -0.5, 0.375, ((0, 4), (1, 8)), jnp.float32),
        "left_tiles": with_ends(jax.random.randint(streams_of[3], (NP,), 1, 5), jax.random.fold_in(streams_of[3], 1), 1, 4).astype(jnp.int32),
        "right_tiles": with_ends(jax.random.randint(streams_of[4], (NQ,), 1, 5), jax.random.fold_in(streams_of[4], 1), 1, 4).astype(jnp.int32),
        "pairs": with_ends(jax.random.randint(streams_of[5], (KP, 2), 0, NW), jax.random.fold_in(streams_of[5], 1), 0, NW - 1).astype(jnp.int32),
        "coefs": bell_draw(streams_of[6], (KP,), 0.15, 2.0, (), jnp.float32),
    }


def reference(theta, left_env, right_env, left_tiles, right_tiles, pairs, coefs):
    quarter = MB // 4
    cells = jnp.arange(MB).astype(jnp.int32)
    left_mask = (cells[None, :] < quarter * left_tiles[:, None]).astype(jnp.float32)
    right_mask = (cells[None, :] < quarter * right_tiles[:, None]).astype(jnp.float32)
    masked = theta * left_mask[:, None, :, None] * right_mask[None, :, None, :]
    bonds = jnp.arange(NW).astype(jnp.int32)
    onehot_left = (pairs[:, 0][:, None] == bonds[None, :]).astype(jnp.float32)
    onehot_right = (pairs[:, 1][:, None] == bonds[None, :]).astype(jnp.float32)
    couplings = jnp.einsum("ka,kb->ab", onehot_left * coefs[:, None], onehot_right, precision=lax.Precision.HIGHEST)
    dressed = jnp.einsum("ab,bqij->aqij", couplings, right_env, precision=lax.Precision.HIGHEST)

    def per_left(index):
        panel = left_env[:, index]
        blocks = masked[index]
        partial_value = jnp.einsum("aij,qjk->aqik", panel, blocks, precision=lax.Precision.HIGHEST)
        return jnp.einsum("aqik,aqlk->qil", partial_value, dressed, precision=lax.Precision.HIGHEST)

    summed = lax.map(per_left, jnp.arange(NP).astype(jnp.int32))
    return summed * left_mask[:, None, :, None] * right_mask[None, :, None, :]
```

```python
import functools

import jax
import jax.numpy as jnp
from jax import lax
from jax.experimental import pallas as pl
from jax.experimental.pallas import tpu as pltpu
from jax.sharding import PartitionSpec as P

F32 = jnp.float32
BF16 = jnp.bfloat16
VMEM = pl.BlockSpec(memory_space=pltpu.VMEM)
SMEM = pl.BlockSpec(memory_space=pltpu.SMEM)


def split(value):
    high = value.astype(BF16)
    return high, (value - high.astype(F32)).astype(BF16)


def product(left, right, dims):
    def one(a, b):
        return lax.dot_general(a, b, (dims, ((), ())), preferred_element_type=F32)

    return one(left[0], right[0]) + (one(left[0], right[1]) + one(left[1], right[0]))


def dress_kernel(order, place, couplings, *refs):
    parts, out = refs[:-1], refs[-1]
    count = out.shape[0]
    rows = out.shape[1]
    step = 8
    row_at = place[0]

    def body(i, _):
        at = pl.ds(pl.multiple_of(i * step, step), step)
        totals = [jnp.zeros((step, out.shape[2]), F32) for _ in range(count)]
        for part, shift in zip(parts, order):
            base = (row_at ^ shift) * count
            for a in range(count):
                value = part[a, at, :]
                for b in range(count):
                    totals[b] += couplings[base + a, row_at * count + b] * value
        for b in range(count):
            out[b, at, :] = totals[b]
        return 0

    lax.fori_loop(0, rows // step, body, 0)


def dress(order, place, couplings, parts):
    size = parts[0].size
    return pl.pallas_call(
        functools.partial(dress_kernel, order),
        out_shape=jax.ShapeDtypeStruct(parts[0].shape, F32),
        in_specs=[SMEM, SMEM] + [VMEM] * len(parts),
        out_specs=VMEM,
        cost_estimate=pl.CostEstimate(
            flops=8 * size * len(parts), bytes_accessed=4 * size * (len(parts) + 1), transcendentals=0
        ),
        name="dress",
    )(place, couplings, *parts)


def pair_kernel(keep_shifts, send_shifts, place, tiles, left, theta, *refs):
    rights, keep, send, work = refs[:-3], refs[-3], refs[-2], refs[-1]
    bonds, size = left.shape[0], left.shape[1]
    slab = keep.shape[2]
    quarter = size // 4
    row_at = place[0]
    rows = lax.broadcasted_iota(jnp.int32, (size, size), 0)
    columns = lax.broadcasted_iota(jnp.int32, (size, size), 1)
    in_left = rows < quarter * tiles[0]
    for at, right in enumerate(rights):
        in_right = columns < quarter * tiles[1 + at]
        inside = jnp.logical_and(in_left, in_right)
        masked = split(jnp.where(inside, theta[tiles[1 + len(rights) + at]], 0.0))
        total = jnp.zeros((size, size), F32)
        for b in range(bonds):
            partial_value = split(product(split(left[b]), masked, ((1,), (0,))))
            total += product(partial_value, split(right[b]), ((1,), (1,)))
        work[...] = jnp.where(inside, total, 0.0)
        for out, shifts in ((keep, keep_shifts), (send, send_shifts)):
            for j, shift in enumerate(shifts):
                begin = pl.multiple_of((row_at ^ shift) * slab, slab)
                out[j, at] = work[pl.ds(begin, slab), :]


def pair_products(keep_shifts, send_shifts, place, tiles, left, theta, rights, slab):
    size = left.shape[1]
    count = len(rights)
    shapes = [
        jax.ShapeDtypeStruct((len(s), count, slab, size), F32) for s in (keep_shifts, send_shifts)
    ]
    bonds = left.shape[0]
    return pl.pallas_call(
        functools.partial(pair_kernel, keep_shifts, send_shifts),
        out_shape=shapes,
        in_specs=[SMEM, SMEM] + [VMEM] * (2 + count),
        out_specs=[VMEM, VMEM],
        scratch_shapes=[pltpu.VMEM((size, size), F32)],
        cost_estimate=pl.CostEstimate(
            flops=12 * count * bonds * size**3,
            bytes_accessed=4 * (left.size + theta.size + count * left.size * 2),
            transcendentals=0,
        ),
        name="pair",
    )(place, tiles, left, theta, *rights)


def place_kernel(index, mine, mine_more, other, out):
    count = mine.shape[0]
    for j in range(count):
        out[0, index[j]] = mine[j] + mine_more[j]
        out[0, index[count + j]] = other[j]


def finish(index, mine, mine_more, other):
    count, slab, size = mine.shape
    return pl.pallas_call(
        place_kernel,
        out_shape=jax.ShapeDtypeStruct((1, 2 * count, slab, size), F32),
        in_specs=[SMEM, VMEM, VMEM, VMEM],
        out_specs=VMEM,
        cost_estimate=pl.CostEstimate(flops=mine.size, bytes_accessed=20 * mine.size, transcendentals=0),
        name="finish",
    )(index, mine, mine_more, other)


def per_device(rows, blks, theta, left_env, right_env, left_tiles, right_tiles, pairs, coefs):
    bonds_here = left_env.shape[0]
    bond_total = bonds_here * rows
    size = theta.shape[2]
    slab = size // rows
    inner = blks // 4
    row_at = lax.axis_index("row")
    blk_at = lax.axis_index("blk")
    high, low, x_at = blk_at // (2 * inner), (blk_at // inner) % 2, blk_at % inner

    def by_row(value, shift):
        return lax.ppermute(value, "row", [(r, r ^ shift) for r in range(rows)])

    def by_blk(value, target):
        moves = []
        for h in range(2):
            for l in range(2):
                for x in range(inner):
                    a, b, c = target(h, l, x)
                    moves.append(((h * 2 + l) * inner + x, (a * 2 + b) * inner + c))
        return lax.ppermute(value, "blk", moves)

    bits = []
    while 1 << len(bits) < rows:
        bits.append(1 << len(bits))

    bonds = jnp.arange(bond_total)
    onehot_left = (pairs[:, 0][:, None] == bonds[None, :]).astype(F32)
    onehot_right = (pairs[:, 1][:, None] == bonds[None, :]).astype(F32)
    couplings = jnp.einsum(
        "ka,kb->ab", onehot_left * coefs[:, None], onehot_right, precision=lax.Precision.HIGHEST
    )

    parts, order = [left_env[:, 0]], [0]
    for bit in reversed(bits):
        parts += [by_row(part, bit) for part in parts]
        order += [shift ^ bit for shift in order]

    right = right_env[:, 0]
    second = by_blk(right, lambda h, l, x: ((l + 1) % 2, h, x))
    first = by_blk(right, lambda h, l, x: (l, h, x))
    slots = []
    for value in (second, first):
        slots.append(
            [value]
            + [by_blk(value, lambda h, l, x, s=s: (h, l, (x + s) % inner)) for s in range(1, inner)]
        )
    shift_of = (1, 0)

    count = 2 * inner
    theta_own = lax.dynamic_slice_in_dim(theta[0], low * count, count, 0)
    theta_other = by_blk(
        lax.dynamic_slice_in_dim(theta[0], (1 - low) * count, count, 0),
        lambda h, l, x: (h, 1 - l, x),
    )
    place = jnp.stack([row_at]).astype(jnp.int32)
    dressed = dress(order, place, couplings, parts)
    dressed_other = by_blk(dressed, lambda h, l, x: (h, 1 - l, x))

    partner = (high * 2 + 1 - low) * inner + x_at
    local = [
        ((high + shift_of[k]) % 2) * inner + (x_at - s) % inner for k in range(2) for s in range(inner)
    ]
    local = jnp.stack(local).astype(jnp.int32)
    tiles_right = right_tiles[low * count + local]
    keep_shifts = [s for s in range(rows) if s & 1 == 0]
    send_shifts = [s for s in range(rows) if s & 1 == 1]

    def block(p, left, thetas):
        made = []
        for k in range(2):
            at = slice(k * inner, (k + 1) * inner)
            tiles = jnp.concatenate([left_tiles[p][None], tiles_right[at], local[at]])
            keep, send = pair_products(
                keep_shifts, send_shifts, place, tiles, left, thetas, slots[k], slab
            )
            made.append((keep, by_row(send, 1)))
        return made

    def reduce_rows(made):
        keep = jnp.concatenate([keep + got for keep, got in made], axis=1)
        for bit in bits[1:]:
            kept, gone = keep[0::2], keep[1::2]
            sent = by_row(gone, bit)
            if bit == bits[-1]:
                return kept[0], sent[0]
            keep = kept + sent
        return keep[0], jnp.zeros_like(keep[0])

    other_keep, other_sent = reduce_rows(block(partner, dressed_other, theta_other))
    back = by_blk(other_keep + other_sent, lambda h, l, x: (h, 1 - l, x))
    own_keep, own_sent = reduce_rows(block(blk_at, dressed, theta_own))
    index = jnp.concatenate([low * count + local, (1 - low) * count + local]).astype(jnp.int32)
    return finish(index, own_keep, own_sent, back)


def solution(mesh):
    return jax.shard_map(
        functools.partial(per_device, mesh.shape["row"], mesh.shape["blk"]),
        mesh=mesh,
        in_specs=(
            P("blk", None, None, None),
            P("row", "blk", None, None),
            P("row", "blk", None, None),
            P(),
            P(),
            P(),
            P(),
        ),
        out_specs=P("blk", None, "row", None),
        check_vma=False,
    )
```

```python
import functools

import jax
import jax.numpy as jnp
from jax import lax
from jax.experimental import pallas as pl
from jax.experimental.pallas import tpu as pltpu
from jax.sharding import PartitionSpec as P


F32 = jnp.float32
BF16 = jnp.bfloat16
VMEM = pl.BlockSpec(memory_space=pltpu.VMEM)
SMEM = pl.BlockSpec(memory_space=pltpu.SMEM)
ANY = pl.BlockSpec(memory_space=pl.ANY)


def split(value):
    high = value.astype(BF16)
    return high, (value - high.astype(F32)).astype(BF16)


def product(left, right, dims):
    def one(a, b):
        return lax.dot_general(a, b, (dims, ((), ())), preferred_element_type=F32)

    return one(left[0], right[0]) + (one(left[0], right[1]) + one(left[1], right[0]))


def dress_kernel(shifts, rows, info, couplings, *refs):
    parts, rest = refs[: len(shifts)], refs[len(shifts) :]
    outs, before = rest[-2:], rest[:-2]
    half = rows // 2
    row = info[0]
    count, size = outs[0].shape[0], outs[0].shape[2]
    slab = size // rows
    chunk = min(32, slab)
    factors = [
        [[couplings[(row ^ shift) * count + a, row * count + b] for b in range(count)] for a in range(count)]
        for shift in shifts
    ]
    for kind in range(2):
        for j in range(half):
            begin = (row ^ (2 * j + 1 - kind)) * slab
            for c in range(slab // chunk):
                at = pl.ds(pl.multiple_of(begin + c * chunk, chunk), chunk)
                to = pl.ds(j * slab + c * chunk, chunk)
                totals = [before[kind][b, to, :] if before else None for b in range(count)]
                for part, by in zip(parts, factors):
                    for a in range(count):
                        value = part[a, at, :]
                        for b in range(count):
                            term = by[a][b] * value
                            totals[b] = term if totals[b] is None else totals[b] + term
                for b in range(count):
                    outs[kind][b, to, :] = totals[b]


def dress(shifts, rows, info, couplings, parts, before=()):
    count, size, _ = parts[0].shape
    shape = jax.ShapeDtypeStruct((count, size // 2, size), F32)
    return pl.pallas_call(
        functools.partial(dress_kernel, shifts, rows),
        out_shape=[shape, shape],
        in_specs=[SMEM, SMEM] + [VMEM] * (len(parts) + len(before)),
        out_specs=[VMEM, VMEM],
        cost_estimate=pl.CostEstimate(
            flops=8 * parts[0].size * len(parts),
            bytes_accessed=4 * parts[0].size * (len(parts) + 2),
            transcendentals=0,
        ),
        name="dress",
    )(info, couplings, *parts, *before)


def pair_kernel(spec, info, left_tiles, right_tiles, *refs):
    rows, inner, n_in, jobs, kinds, slots = spec
    ins, outs = refs[:n_in], dict(zip(kinds, refs[n_in : n_in + len(kinds)]))
    held = refs[n_in + len(kinds) : -2]
    thetas, sem = refs[-2], refs[-1]
    row, high, low, x_at = info[0], info[1], info[2], info[3]
    size = thetas.shape[-1]
    quarter = size // 4
    width = size // 2
    count = 2 * inner
    slab = size // rows
    half = rows // 2

    def local_of(k, s):
        return ((high + k) % 2) * inner + (x_at + inner - s) % inner

    copies, theta_copies = {}, []
    for lefts, theta_at, relative, foreign, pieces in jobs:
        for i in [i for i, _ in lefts]:
            if i not in copies:
                copies[i] = pltpu.make_async_copy(ins[i], held[slots[i]], sem.at[i])
                copies[i].start()
        for k, s, _, rights in pieces:
            local = local_of(k, s)
            if relative:
                per = count // rows
                place = ((local // per) ^ row) * per + local % per
            else:
                place = low * count + local
            n = len(theta_copies)
            theta_copies.append(
                pltpu.make_async_copy(ins[theta_at].at[place], thetas.at[n], sem.at[n_in + n])
            )
            theta_copies[n].start()
            for i in rights:
                if i not in copies:
                    copies[i] = pltpu.make_async_copy(ins[i], held[slots[i]], sem.at[i])
                    copies[i].start()
    waited = set()

    def ready(i):
        if i not in waited:
            copies[i].wait()
            waited.add(i)
        return held[slots[i]]

    made = {kind: 0 for kind in kinds}
    n = 0
    for lefts, _, relative, foreign, pieces in jobs:
        tile = left_tiles[(2 * high + (1 - low if foreign else low)) * inner + x_at]
        depth = lax.broadcasted_iota(jnp.int32, (size, size), 0)
        wide = lax.broadcasted_iota(jnp.int32, (size, size), 1)
        for k, s, column, rights in pieces:
            limit = quarter * right_tiles[low * count + local_of(k, s)]
            left_refs = [ready(i) for i, _ in lefts]
            theta_copies[n].wait()
            inside = jnp.logical_and(depth < quarter * tile, wide < limit)
            masked = split(jnp.where(inside, thetas[n], 0.0))
            n += 1
            right_refs = [ready(i) for i in rights]
            part = left_refs[0].shape[1]
            columns = sum(r.shape[1] for r in right_refs)
            total = None
            for b in range(left_refs[0].shape[0]):
                left = left_refs[0][b]
                right = right_refs[0][b]
                if len(left_refs) > 1:
                    left = jnp.concatenate([r[b] for r in left_refs], axis=0)
                if len(right_refs) > 1:
                    right = jnp.concatenate([r[b] for r in right_refs], axis=0)
                partial_value = split(product(split(left), masked, ((1,), (0,))))
                term = product(partial_value, split(right), ((1,), (1,)))
                total = term if total is None else total + term
            in_right = lax.broadcasted_iota(jnp.int32, (slab, columns), 1) + column < limit
            at_row = lax.broadcasted_iota(jnp.int32, (slab, columns), 0)
            for at, (_, kind) in enumerate(lefts):
                for j in range(half):
                    shift = 2 * j + 1 if kind == "send" else 2 * j
                    begin = at * part + j * slab
                    value = jnp.where(
                        jnp.logical_and(in_right, at_row + (row ^ shift) * slab < quarter * tile),
                        total[begin : begin + slab],
                        0.0,
                    )
                    for w in range(columns // width):
                        outs[kind][j, made[kind] + w] = value[:, w * width : (w + 1) * width]
                made[kind] += columns // width
    assert len(waited) == len(copies)


def pair_products(rows, inner, scalars, jobs):
    arrays = []

    def index(array):
        for i, known in enumerate(arrays):
            if known is array:
                return i
        arrays.append(array)
        return len(arrays) - 1

    compact, streamed = [], []
    units = {}
    flops, n_thetas = 0, 0
    size = jobs[0][1].shape[-1]
    for lefts, theta, relative, foreign, pieces in jobs:
        lefts_at = tuple((index(a), kind) for a, kind in lefts)
        pieces_at = tuple((k, s, c, tuple(index(r) for r in rights)) for k, s, c, rights in pieces)
        compact.append((lefts_at, index(theta), relative, foreign, pieces_at))
        streamed += [i for i, _ in lefts_at] + [i for piece in pieces_at for i in piece[3]]
        n_thetas += len(pieces)
        for _, kind in lefts:
            units[kind] = units.get(kind, 0) + sum(r.shape[1] for p in pieces for r in p[3]) // (size // 2)
        flops += 12 * len(lefts) * len(pieces) * lefts[0][0].size * size
    streamed = sorted(set(streamed))
    slots = {i: n for n, i in enumerate(streamed)}
    kinds = tuple(units)
    out = pl.pallas_call(
        functools.partial(pair_kernel, (rows, inner, len(arrays), tuple(compact), kinds, slots)),
        out_shape=[
            jax.ShapeDtypeStruct((rows // 2, units[kind], size // rows, size // 2), F32) for kind in kinds
        ],
        in_specs=[SMEM] * 3 + [ANY] * len(arrays),
        out_specs=[VMEM] * len(kinds),
        scratch_shapes=[pltpu.VMEM(arrays[i].shape, F32) for i in streamed]
        + [pltpu.VMEM((n_thetas, size, size), F32), pltpu.SemaphoreType.DMA((len(arrays) + n_thetas,))],
        cost_estimate=pl.CostEstimate(
            flops=flops, bytes_accessed=4 * sum(arrays[i].size for i in streamed), transcendentals=0
        ),
        name="pair",
    )(*scalars, *arrays)
    return dict(zip(kinds, out))


def finish_kernel(inner, units, info, *refs):
    out = refs[-1]
    high, low, x_at = info[1], info[2], info[3]
    count = 2 * inner
    at = 0
    for foreign, terms, listed in units:
        for u, (k, s, w) in enumerate(listed):
            local = ((high + k) % 2) * inner + (x_at + inner - s) % inner
            index = (1 - low if foreign else low) * count + local
            value = refs[at][u]
            for t in range(1, terms):
                value = value + refs[at + t][u]
            width = value.shape[1]
            out[0, index, :, w * width : (w + 1) * width] = value
        at += terms


def finish(inner, info, groups, slab, size):
    arrays = [a for _, terms, _ in groups for a in terms]
    units = tuple((foreign, len(terms), tuple(listed)) for foreign, terms, listed in groups)
    return pl.pallas_call(
        functools.partial(finish_kernel, inner, units),
        out_shape=jax.ShapeDtypeStruct((1, 4 * inner, slab, size), F32),
        in_specs=[SMEM] + [VMEM] * len(arrays),
        out_specs=VMEM,
        cost_estimate=pl.CostEstimate(
            flops=4 * inner * slab * size, bytes_accessed=16 * inner * slab * size * 2, transcendentals=0
        ),
        name="finish",
    )(info, *arrays)


def per_device(rows, blks, theta, left_env, right_env, left_tiles, right_tiles, pairs, coefs):
    bond_total = left_env.shape[0] * rows
    size = theta.shape[2]
    slab = size // rows
    inner = blks // 4
    count = 2 * inner
    row = lax.axis_index("row")
    blk = lax.axis_index("blk")
    high, low, x_at = blk // count, (blk // inner) % 2, blk % inner
    info = jnp.stack([row, high, low, x_at]).astype(jnp.int32)
    scalars = (info, left_tiles, right_tiles)

    def by_row(value, shift):
        return lax.ppermute(value, "row", [(r, r ^ shift) for r in range(rows)])

    def by_blk(value, target):
        moves = []
        for h in range(2):
            for l in range(2):
                for x in range(inner):
                    a, b, c = target(h, l, x)
                    if (a, b, c) != (h, l, x):
                        moves.append(((h * 2 + l) * inner + x, (a * 2 + b) * inner + c))
        return lax.ppermute(value, "blk", moves)

    def partner(h, l, x):
        return h, 1 - l, x

    def gather_inner(value):
        return [value] + [by_blk(value, lambda h, l, x, s=s: (h, l, (x + s) % inner)) for s in range(1, inner)]

    left, right = left_env[:, 0], right_env[:, 0]
    halves = lax.optimization_barrier((right[:, : size // 2], right[:, size // 2 :]))

    bits = []
    while 1 << len(bits) < rows:
        bits.append(1 << len(bits))
    far, far_order = [left], [0]
    for bit in reversed(bits[1:]):
        far += [by_row(part, bit) for part in far]
        far_order += [s ^ bit for s in far_order]
    near = [by_row(left, 1)]

    def second_of(h, l, x):
        return (l + 1) % 2, h, x

    def first_of(h, l, x):
        return l, h, x

    per = count // rows
    theta_other = lax.dynamic_slice_in_dim(theta[0], (1 - low) * count + row * per, per, 0)
    theta_parts = [by_blk(theta_other, partner)]
    theta_order = [0]

    second_a = by_blk(halves[0], second_of)

    bonds = jnp.arange(bond_total)
    onehot_left = (pairs[:, 0][:, None] == bonds[None, :]).astype(F32)
    onehot_right = (pairs[:, 1][:, None] == bonds[None, :]).astype(F32)
    couplings = jnp.einsum(
        "ka,kb->ab", onehot_left * coefs[:, None], onehot_right, precision=lax.Precision.HIGHEST
    )
    early = dress([0, 1], rows, info, couplings, [left] + near)

    second_b = by_blk(halves[1], second_of)
    second_xa = gather_inner(second_a)
    for bit in reversed(bits[1:]):
        theta_parts += [by_row(t, bit) for t in theta_parts]
        theta_order += [s ^ bit for s in theta_order]
    crossed = [by_row(part, 1) for part in far[1:]]
    shifts = far_order[1:] + [s ^ 1 for s in far_order[1:]]
    dressed = dress(shifts, rows, info, couplings, far[1:] + crossed, early)
    dressed_other = [by_blk(dressed[0], partner), by_blk(dressed[1], partner)]

    moved_a = by_blk(halves[0], first_of)
    first_a = jnp.where(high == low, halves[0], moved_a)
    second_xb = gather_inner(second_b)
    theta_cross = by_row(jnp.concatenate(theta_parts), 1)
    moved_b = by_blk(halves[1], first_of)
    first_b = jnp.where(high == low, halves[1], lax.optimization_barrier((moved_b, first_a))[0])
    first_xa = gather_inner(first_a)
    first_xb = gather_inner(first_b)
    whole = {}
    for n, s in enumerate(theta_order):
        whole[s] = theta_parts[n]
        whole[s ^ 1] = theta_cross[n * per : (n + 1) * per]
    thetas_other = jnp.concatenate([whole[s] for s in range(rows)])

    own = [(dressed[0], "send"), (dressed[1], "keep")]
    their = [(dressed_other[0], "send"), (dressed_other[1], "keep")]
    seconds = [(1, s, 0, [second_xa[s], second_xb[s]]) for s in range(inner)]
    firsts = [(0, 0, 0, [first_a, first_b])]
    own_firsts = firsts + [(0, s, 0, [first_xa[s]]) for s in range(1, inner)]
    own_lasts = [(0, s, size // 2, [first_xb[s]]) for s in range(1, inner)]
    their_lasts = [(0, s, 0, [first_xa[s], first_xb[s]]) for s in range(1, inner)]

    def pairs_of(*jobs):
        return pair_products(rows, inner, scalars, list(jobs))

    own1 = pairs_of((own, theta[0], False, False, seconds))
    own1_got = by_row(own1["send"], 1)
    for1 = pairs_of((their, thetas_other, True, True, seconds + firsts))
    for1_got = by_row(for1["send"], 1)
    own2 = pairs_of((own, theta[0], False, False, own_firsts))
    own2_got = by_row(own2["send"], 1)
    last = pairs_of((their, thetas_other, True, True, their_lasts), (own, theta[0], False, False, own_lasts))
    last_got = by_row(last["send"], 1)

    def over_rows(value):
        for bit in bits[1:]:
            kept, gone = value[0::2], value[1::2]
            got = by_row(gone, bit)
            if bit == bits[-1]:
                return kept[0], got[0]
            value = kept + got
        return value[0], jnp.zeros_like(value[0])

    their_kept, their_got = over_rows(for1["keep"] + for1_got)
    own_kept, own_got = over_rows(jnp.concatenate([own1["keep"] + own1_got, own2["keep"] + own2_got], axis=1))
    back = by_blk(their_kept + their_got, partner)
    last_kept, last_other = over_rows(last["keep"] + last_got)
    n_last = 2 * len(their_lasts)
    last_back = by_blk(last_kept[:n_last] + last_other[:n_last], partner)

    units = [(1, s, w) for s in range(inner) for w in range(2)] + [(0, 0, 0), (0, 0, 1)]
    own_units = units + [(0, s, 0) for s in range(1, inner)]
    groups = [
        (False, [own_kept, own_got], own_units),
        (False, [last_kept[n_last:], last_other[n_last:]], [(0, s, 1) for s in range(1, inner)]),
        (True, [back], units),
        (True, [last_back], [(0, s, w) for s in range(1, inner) for w in range(2)]),
    ]
    return finish(inner, info, groups, slab, size)


def solution(mesh):
    def body(*args):
        return per_device(mesh.shape["row"], mesh.shape["blk"], *args)

    return jax.shard_map(
        body,
        mesh=mesh,
        in_specs=(
            P("blk", None, None, None),
            P("row", "blk", None, None),
            P("row", "blk", None, None),
            P(),
            P(),
            P(),
            P(),
        ),
        out_specs=P("blk", None, "row", None),
        check_vma=False,
    )
```

```python
import functools

import jax
import jax.numpy as jnp
from jax import lax
from jax.experimental import pallas as pl
from jax.experimental.pallas import tpu as pltpu
from jax.sharding import PartitionSpec as P


F32 = jnp.float32
BF16 = jnp.bfloat16
VMEM = pl.BlockSpec(memory_space=pltpu.VMEM)
SMEM = pl.BlockSpec(memory_space=pltpu.SMEM)


def split(value):
    high = value.astype(BF16)
    return high, (value - high.astype(F32)).astype(BF16)


def grant(arrays, shapes):
    size = 4 * sum(a.size for a in list(arrays) + list(shapes)) + (8 << 20)
    return pltpu.CompilerParams(vmem_limit_bytes=min(size, 60 << 20))


def product(left, right, dims):
    def one(a, b):
        return lax.dot_general(a, b, (dims, ((), ())), preferred_element_type=F32)

    return one(left[0], right[0]) + (one(left[0], right[1]) + one(left[1], right[0]))


def dress_kernel(shifts, rows, info, couplings, *refs):
    parts, rest = refs[: len(shifts)], refs[len(shifts) :]
    outs, before = rest[-2:], rest[:-2]
    half = rows // 2
    row = info[0]
    count, size = outs[0].shape[0], outs[0].shape[2]
    slab = size // rows
    chunk = min(32, slab)
    factors = [
        [[couplings[(row ^ shift) * count + a, row * count + b] for b in range(count)] for a in range(count)]
        for shift in shifts
    ]
    for kind in range(2):
        for j in range(half):
            begin = (row ^ (2 * j + 1 - kind)) * slab
            for c in range(slab // chunk):
                at = pl.ds(pl.multiple_of(begin + c * chunk, chunk), chunk)
                to = pl.ds(j * slab + c * chunk, chunk)
                totals = [before[kind][b, to, :] if before else None for b in range(count)]
                for part, by in zip(parts, factors):
                    for a in range(count):
                        value = part[a, at, :]
                        for b in range(count):
                            term = by[a][b] * value
                            totals[b] = term if totals[b] is None else totals[b] + term
                for b in range(count):
                    outs[kind][b, to, :] = totals[b]


def dress(shifts, rows, info, couplings, parts, before=()):
    count, size, _ = parts[0].shape
    shape = jax.ShapeDtypeStruct((count, size // 2, size), F32)
    return pl.pallas_call(
        functools.partial(dress_kernel, shifts, rows),
        out_shape=[shape, shape],
        in_specs=[SMEM, SMEM] + [VMEM] * (len(parts) + len(before)),
        out_specs=[VMEM, VMEM],
        compiler_params=grant(list(parts) + list(before), [shape, shape]),
        cost_estimate=pl.CostEstimate(
            flops=8 * parts[0].size * len(parts),
            bytes_accessed=4 * parts[0].size * (len(parts) + 2),
            transcendentals=0,
        ),
        name="dress",
    )(info, couplings, *parts, *before)


def pair_kernel(spec, info, left_tiles, right_tiles, *refs):
    rows, inner, n_in, jobs, kinds = spec
    ins, outs = refs[:n_in], dict(zip(kinds, refs[n_in:]))
    row, high, low, x_at = info[0], info[1], info[2], info[3]
    size = ins[0].shape[-1]
    quarter = size // 4
    width = size // 2
    count = 2 * inner
    slab = size // rows
    half = rows // 2

    def local_of(k, s):
        return ((high + k) % 2) * inner + (x_at + inner - s) % inner

    made = {kind: 0 for kind in kinds}
    for lefts, theta_at, relative, foreign, pieces in jobs:
        tile = left_tiles[(2 * high + (1 - low if foreign else low)) * inner + x_at]
        depth = lax.broadcasted_iota(jnp.int32, (size, size), 0)
        wide = lax.broadcasted_iota(jnp.int32, (size, size), 1)
        for k, s, column, rights in pieces:
            local = local_of(k, s)
            limit = quarter * right_tiles[low * count + local]
            if relative:
                per = count // rows
                place = ((local // per) ^ row) * per + local % per
            else:
                place = low * count + local
            left_refs = [ins[i] for i, _ in lefts]
            inside = jnp.logical_and(depth < quarter * tile, wide < limit)
            masked = split(jnp.where(inside, ins[theta_at][place], 0.0))
            right_refs = [ins[i] for i in rights]
            part = left_refs[0].shape[1]
            columns = sum(r.shape[1] for r in right_refs)
            total = None
            for b in range(left_refs[0].shape[0]):
                left = left_refs[0][b]
                right = right_refs[0][b]
                if len(left_refs) > 1:
                    left = jnp.concatenate([r[b] for r in left_refs], axis=0)
                if len(right_refs) > 1:
                    right = jnp.concatenate([r[b] for r in right_refs], axis=0)
                partial_value = split(product(split(left), masked, ((1,), (0,))))
                term = product(partial_value, split(right), ((1,), (1,)))
                total = term if total is None else total + term
            in_right = lax.broadcasted_iota(jnp.int32, (slab, columns), 1) + column < limit
            at_row = lax.broadcasted_iota(jnp.int32, (slab, columns), 0)
            for at, (_, kind) in enumerate(lefts):
                for j in range(half):
                    shift = 2 * j + 1 if kind == "send" else 2 * j
                    begin = at * part + j * slab
                    value = jnp.where(
                        jnp.logical_and(in_right, at_row + (row ^ shift) * slab < quarter * tile),
                        total[begin : begin + slab],
                        0.0,
                    )
                    for w in range(columns // width):
                        outs[kind][j, made[kind] + w] = value[:, w * width : (w + 1) * width]
                made[kind] += columns // width


def pair_products(rows, inner, scalars, jobs):
    arrays = []

    def index(array):
        for i, known in enumerate(arrays):
            if known is array:
                return i
        arrays.append(array)
        return len(arrays) - 1

    compact = []
    units = {}
    flops = 0
    size = jobs[0][1].shape[-1]
    for lefts, theta, relative, foreign, pieces in jobs:
        lefts_at = tuple((index(a), kind) for a, kind in lefts)
        pieces_at = tuple((k, s, c, tuple(index(r) for r in rights)) for k, s, c, rights in pieces)
        compact.append((lefts_at, index(theta), relative, foreign, pieces_at))
        for _, kind in lefts:
            units[kind] = units.get(kind, 0) + sum(r.shape[1] for p in pieces for r in p[3]) // (size // 2)
        flops += 12 * len(lefts) * len(pieces) * lefts[0][0].size * size
    kinds = tuple(units)
    shapes = [
        jax.ShapeDtypeStruct((rows // 2, units[kind], size // rows, size // 2), F32) for kind in kinds
    ]
    out = pl.pallas_call(
        functools.partial(pair_kernel, (rows, inner, len(arrays), tuple(compact), kinds)),
        out_shape=shapes,
        in_specs=[SMEM] * 3 + [VMEM] * len(arrays),
        out_specs=[VMEM] * len(kinds),
        compiler_params=grant(arrays, shapes),
        cost_estimate=pl.CostEstimate(
            flops=flops, bytes_accessed=4 * sum(a.size for a in arrays), transcendentals=0
        ),
        name="pair",
    )(*scalars, *arrays)
    return dict(zip(kinds, out))


def finish_kernel(inner, units, info, *refs):
    out = refs[-1]
    high, low, x_at = info[1], info[2], info[3]
    count = 2 * inner
    at = 0
    for foreign, terms, listed in units:
        for u, (k, s, w) in enumerate(listed):
            local = ((high + k) % 2) * inner + (x_at + inner - s) % inner
            index = (1 - low if foreign else low) * count + local
            value = refs[at][u]
            for t in range(1, terms):
                value = value + refs[at + t][u]
            width = value.shape[1]
            out[0, index, :, w * width : (w + 1) * width] = value
        at += terms


def finish(inner, info, groups, slab, size):
    arrays = [a for _, terms, _ in groups for a in terms]
    units = tuple((foreign, len(terms), tuple(listed)) for foreign, terms, listed in groups)
    shape = jax.ShapeDtypeStruct((1, 4 * inner, slab, size), F32)
    return pl.pallas_call(
        functools.partial(finish_kernel, inner, units),
        out_shape=shape,
        compiler_params=grant(arrays, [shape]),
        in_specs=[SMEM] + [VMEM] * len(arrays),
        out_specs=VMEM,
        cost_estimate=pl.CostEstimate(
            flops=4 * inner * slab * size, bytes_accessed=16 * inner * slab * size * 2, transcendentals=0
        ),
        name="finish",
    )(info, *arrays)


def per_device(rows, blks, theta, left_env, right_env, left_tiles, right_tiles, pairs, coefs):
    bond_total = left_env.shape[0] * rows
    size = theta.shape[2]
    slab = size // rows
    inner = blks // 4
    count = 2 * inner
    row = lax.axis_index("row")
    blk = lax.axis_index("blk")
    high, low, x_at = blk // count, (blk // inner) % 2, blk % inner
    info = jnp.stack([row, high, low, x_at]).astype(jnp.int32)
    scalars = (info, left_tiles, right_tiles)

    def by_row(value, shift):
        return lax.ppermute(value, "row", [(r, r ^ shift) for r in range(rows)])

    def by_blk(value, target):
        moves = []
        for h in range(2):
            for l in range(2):
                for x in range(inner):
                    a, b, c = target(h, l, x)
                    if (a, b, c) != (h, l, x):
                        moves.append(((h * 2 + l) * inner + x, (a * 2 + b) * inner + c))
        return lax.ppermute(value, "blk", moves)

    def partner(h, l, x):
        return h, 1 - l, x

    def gather_inner(value):
        return [value] + [by_blk(value, lambda h, l, x, s=s: (h, l, (x + s) % inner)) for s in range(1, inner)]

    left, right = left_env[:, 0], right_env[:, 0]
    halves = lax.optimization_barrier((right[:, : size // 2], right[:, size // 2 :]))

    bits = []
    while 1 << len(bits) < rows:
        bits.append(1 << len(bits))
    far, far_order = [left], [0]
    for bit in reversed(bits[1:]):
        far += [by_row(part, bit) for part in far]
        far_order += [s ^ bit for s in far_order]
    near = [by_row(left, 1)]

    def second_of(h, l, x):
        return (l + 1) % 2, h, x

    def first_of(h, l, x):
        return l, h, x

    per = count // rows
    theta_other = lax.dynamic_slice_in_dim(theta[0], (1 - low) * count + row * per, per, 0)
    theta_parts = [by_blk(theta_other, partner)]
    theta_order = [0]

    second_a = by_blk(halves[0], second_of)

    bonds = jnp.arange(bond_total)
    onehot_left = (pairs[:, 0][:, None] == bonds[None, :]).astype(F32)
    onehot_right = (pairs[:, 1][:, None] == bonds[None, :]).astype(F32)
    couplings = jnp.einsum(
        "ka,kb->ab", onehot_left * coefs[:, None], onehot_right, precision=lax.Precision.HIGHEST
    )
    early = dress([0, 1], rows, info, couplings, [left] + near)

    second_b = by_blk(halves[1], second_of)
    second_xa = gather_inner(second_a)
    for bit in reversed(bits[1:]):
        theta_parts += [by_row(t, bit) for t in theta_parts]
        theta_order += [s ^ bit for s in theta_order]
    crossed = [by_row(part, 1) for part in far[1:]]
    shifts = far_order[1:] + [s ^ 1 for s in far_order[1:]]
    dressed = dress(shifts, rows, info, couplings, far[1:] + crossed, early)
    dressed_other = [by_blk(dressed[0], partner), by_blk(dressed[1], partner)]

    moved_a = by_blk(halves[0], first_of)
    first_a = jnp.where(high == low, halves[0], moved_a)
    second_xb = gather_inner(second_b)
    theta_cross = by_row(jnp.concatenate(theta_parts), 1)
    moved_b = by_blk(halves[1], first_of)
    first_b = jnp.where(high == low, halves[1], lax.optimization_barrier((moved_b, first_a))[0])
    first_xa = gather_inner(first_a)
    first_xb = gather_inner(first_b)
    whole = {}
    for n, s in enumerate(theta_order):
        whole[s] = theta_parts[n]
        whole[s ^ 1] = theta_cross[n * per : (n + 1) * per]
    thetas_other = jnp.concatenate([whole[s] for s in range(rows)])

    own = [(dressed[0], "send"), (dressed[1], "keep")]
    their = [(dressed_other[0], "send"), (dressed_other[1], "keep")]
    seconds = [(1, s, 0, [second_xa[s], second_xb[s]]) for s in range(inner)]
    firsts = [(0, 0, 0, [first_a, first_b])]
    own_firsts = firsts + [(0, s, 0, [first_xa[s]]) for s in range(1, inner)]
    own_lasts = [(0, s, size // 2, [first_xb[s]]) for s in range(1, inner)]
    their_lasts = [(0, s, 0, [first_xa[s], first_xb[s]]) for s in range(1, inner)]

    def pairs_of(*jobs):
        return pair_products(rows, inner, scalars, list(jobs))

    own1 = pairs_of((own, theta[0], False, False, seconds))
    own1_got = by_row(own1["send"], 1)
    for1 = pairs_of((their, thetas_other, True, True, seconds + firsts))
    for1_got = by_row(for1["send"], 1)
    own2 = pairs_of((own, theta[0], False, False, own_firsts))
    own2_got = by_row(own2["send"], 1)
    last = pairs_of((their, thetas_other, True, True, their_lasts), (own, theta[0], False, False, own_lasts))
    last_got = by_row(last["send"], 1)

    def over_rows(value):
        for bit in bits[1:]:
            kept, gone = value[0::2], value[1::2]
            got = by_row(gone, bit)
            if bit == bits[-1]:
                return kept[0], got[0]
            value = kept + got
        return value[0], jnp.zeros_like(value[0])

    their_kept, their_got = over_rows(for1["keep"] + for1_got)
    own_kept, own_got = over_rows(jnp.concatenate([own1["keep"] + own1_got, own2["keep"] + own2_got], axis=1))
    back = by_blk(their_kept + their_got, partner)
    last_kept, last_other = over_rows(last["keep"] + last_got)
    n_last = 2 * len(their_lasts)
    last_back = by_blk(last_kept[:n_last] + last_other[:n_last], partner)

    units = [(1, s, w) for s in range(inner) for w in range(2)] + [(0, 0, 0), (0, 0, 1)]
    own_units = units + [(0, s, 0) for s in range(1, inner)]
    groups = [
        (False, [own_kept, own_got], own_units),
        (False, [last_kept[n_last:], last_other[n_last:]], [(0, s, 1) for s in range(1, inner)]),
        (True, [back], units),
        (True, [last_back], [(0, s, w) for s in range(1, inner) for w in range(2)]),
    ]
    return finish(inner, info, groups, slab, size)


def solution(mesh):
    def body(*args):
        return per_device(mesh.shape["row"], mesh.shape["blk"], *args)

    return jax.shard_map(
        body,
        mesh=mesh,
        in_specs=(
            P("blk", None, None, None),
            P("row", "blk", None, None),
            P("row", "blk", None, None),
            P(),
            P(),
            P(),
            P(),
        ),
        out_specs=P("blk", None, "row", None),
        check_vma=False,
    )
```
